512 devices in a mesh: cell: 64 (over x, z), col: 8 (over y, core).
Axes of the slice: x: 4, y: 4, z: 16, core: 2. Of those that a mesh axis runs over, the one named last changes fastest.
Arguments:
- panel_block: float32 [32768, 512], P('cell', 'col'), may hold values from -0.088388348 to 0.088388348, as said below
- trailing: float32 [32768, 7168], P('cell', 'col'), may hold values from -6 to 6
Outputs:
- triangle: float32 [512, 512], replicated
- coupling: float32 [512, 7168], P('cell', 'col')
- projected: float32 [32768, 7168], P('cell', 'col')
The draws below stay inside these ranges and needn't reach their ends.
Inputs may be any that keep to these rules, and one draw needn't show every extreme that they name: `panel_block`: the panel has full column rank.
All inputs are finite; a program needn't handle non-finite values.
Results may differ from the reference program's by a relative error of at most 0.0003.
Values sent between devices are 32-bit elements; how exact they have to be, the bound alone decides.
No kernel may reach another device: no remote copies, remote signals or barrier semaphores. Data moves between devices by JAX's collectives and lax.ppermute only.
A program may use at most 64 MiB of HBM per device.

```python
import jax
import jax.numpy as jnp
from jax import lax

B = 512
MROWS = 32768
TRAIL = 7168


def draw_panel_block(key, part):
    key_a = jax.random.fold_in(key, 11)
    key_b = jax.random.fold_in(key, 12)
    base = jax.random.truncated_normal(key_a, -4.0, 4.0, (MROWS, B), jnp.float32)
    mixed = base + 0.45 * jnp.roll(base, 1, axis=1) + 0.3 * jnp.roll(base, 7, axis=1)
    column_scale = jnp.exp(jax.random.uniform(key_b, (1, B), jnp.float32, 0.0, 1.3862944))
    shaped = jnp.clip(mixed * column_scale, -16.0, 16.0)
    return (shaped * (1.0 / MROWS ** 0.5)).astype(jnp.float32)


def steps_of(own_key, dims, shards, smallest, high):
    loudness, own = 1.0, jax.random.fold_in(own_key, 6)
    for position, parts in shards:
        draws = jnp.exp(jax.random.uniform(jax.random.fold_in(own, position), (parts,), jnp.float32, smallest / len(shards), high / len(shards)))
        loudness = loudness * jnp.repeat(draws, dims[position] // parts).reshape([-1 if axis == position else 1 for axis in range(len(dims))])
    return loudness


def bell_draw(key, dims, deviation, most, split=(), held_as=jnp.bfloat16):
    values = deviation * jax.random.normal(key, dims, jnp.float32)
    if split:
        values = values * steps_of(key, dims, split, -0.22, 0.18)
    return jnp.clip(values, -most, most).astype(held_as)


def setup_inputs(seed: int = 0) -> dict:
    arg_keys = jax.random.split(jax.random.key(seed), 3)
    return {
        "panel_block": draw_panel_block(jax.random.fold_in(arg_keys[2], 71), 0),
        "trailing": bell_draw(arg_keys[1], (MROWS, TRAIL), 1.0, 6.0, ((0, 64), (1, 8)), jnp.float32),
    }


def reference(panel_block, trailing):
    highest = lax.Precision.HIGHEST
    gram = lax.dot_general(panel_block.astype(jnp.float32), panel_block.astype(jnp.float32), (((0,), (0,)), ((), ())), precision=highest, preferred_element_type=jnp.float32)
    lower_factor = jnp.linalg.cholesky(gram)
    basis_t = jax.scipy.linalg.solve_triangular(lower_factor, jnp.transpose(panel_block), lower=True)
    coupling = jnp.dot(basis_t.astype(jnp.float32), trailing.astype(jnp.float32), precision=highest, preferred_element_type=jnp.float32)
    projected = trailing - lax.dot_general(basis_t.astype(jnp.float32), coupling.astype(jnp.float32), (((0,), (0,)), ((), ())), precision=highest, preferred_element_type=jnp.float32)
    return (jnp.transpose(lower_factor), coupling, projected)
```

```python
import functools
import jax, jax.numpy as jnp
from jax import lax
from jax.sharding import Mesh
from jax.sharding import PartitionSpec as P
from jax.experimental import pallas as pl
from jax.experimental.pallas import tpu as pltpu

HI = lax.Precision.HIGHEST
NB = 128

def mxu(a, b, dims):
    return lax.dot_general(a, b, (dims, ((), ())), precision=HI, preferred_element_type=jnp.float32)

def factor_block(s_full, rows_ref):
    G = NB // 8
    sub = lax.broadcasted_iota(jnp.int32, (8, NB), 0)
    lane = lax.broadcasted_iota(jnp.int32, (8, NB), 1)
    s = [s_full[8 * g : 8 * g + 8, :] for g in range(G)]
    v = [jnp.where(lane == sub + 8 * g, 1.0, 0.0).astype(jnp.float32) for g in range(G)]
    for k in range(NB):
        g0, i0 = k // 8, k % 8
        col = [jnp.broadcast_to(s[g][:, k : k + 1], (8, NB)) for g in range(g0, G)]
        r = s[g0][i0 : i0 + 1, :]
        rows_ref[k : k + 1, :] = r
        if k == NB - 1:
            break
        inv = 1.0 / col[0][i0 : i0 + 1, :]
        rd = jnp.broadcast_to(r * inv, (8, NB))
        vd = jnp.broadcast_to(v[g0][i0 : i0 + 1, :] * inv, (8, NB))
        for g in range(g0, G):
            c = col[g - g0]
            if g == g0:
                if i0 == 7:
                    continue
                c = jnp.where(sub > i0, c, 0.0)
            s[g] = s[g] - c * rd
            v[g] = v[g] - c * vd
    return jnp.concatenate(v, axis=0)

def kernel(n, g_ref, r_ref, x_ref, a, rows):
    w = 2 * n
    a[:, :n] = g_ref[...]
    a[:, n:] = jnp.where(lax.broadcasted_iota(jnp.int32, (n, n), 0) == lax.broadcasted_iota(jnp.int32, (n, n), 1), 1.0, 0.0)
    sub = lax.broadcasted_iota(jnp.int32, (NB, NB), 0)
    lane = lax.broadcasted_iota(jnp.int32, (NB, NB), 1)
    wide = lax.broadcasted_iota(jnp.int32, (NB, n), 1)
    high = lax.broadcasted_iota(jnp.int32, (NB, n), 0)

    def step(kb, carry):
        at = pl.multiple_of(kb * NB, NB)
        v = factor_block(a[pl.ds(at, NB), pl.ds(at, NB)], rows)
        rt = rows[...]
        d = jnp.sum(jnp.where(sub == lane, rt, 0.0), axis=1, keepdims=True)
        linv = v * lax.rsqrt(d)
        out = mxu(linv, a[pl.ds(at, NB), :], ((1,), (0,)))
        x_ref[pl.ds(at, NB), :] = out[:, n:]
        r_ref[pl.ds(at, NB), :] = jnp.where(wide >= at + high, out[:, :n], 0.0)
        rm = jnp.where(wide >= at + NB, out[:, :n], 0.0)
        out = jnp.concatenate([rm, out[:, n:]], axis=1)
        a[...] -= mxu(rm, out, ((0,), (0,)))
        return carry

    lax.fori_loop(0, n // NB, step, 0)

def chol_inv(g):
    n = g.shape[0]
    return pl.pallas_call(
        functools.partial(kernel, n),
        out_shape=(jax.ShapeDtypeStruct((n, n), jnp.float32),) * 2,
        in_specs=[pl.BlockSpec(memory_space=pltpu.VMEM)],
        out_specs=[pl.BlockSpec(memory_space=pltpu.VMEM)] * 2,
        scratch_shapes=[pltpu.VMEM((n, 2 * n), jnp.float32), pltpu.VMEM((NB, NB), jnp.float32)],
        compiler_params=pltpu.CompilerParams(vmem_limit_bytes=32 << 20),
    )(g)


def join_cores(part):
    half = part.shape[0] // 2
    both = []
    for block in (part[:half], part[half:]):
        pair = lax.all_gather(block, "core", axis=0, tiled=False)
        both.append(jnp.swapaxes(pair.reshape(2, 2, 64, -1), 0, 1))
    return jnp.concatenate(both, axis=0).reshape(2 * part.shape[0], -1)


def on_device(panel_block, trailing):
    width = trailing.shape[1]
    panel_t = join_cores(
        lax.all_gather(jnp.transpose(panel_block), "y", axis=0, tiled=True)
    )
    partial = jnp.concatenate(
        [
            mxu(panel_t, trailing, ((1,), (0,))),
            mxu(panel_t, panel_block, ((1,), (0,))),
        ],
        axis=1,
    )
    full = partial.shape[1]
    over_x = lax.all_to_all(
        partial.reshape(4, 128, full), "x", 0, 0, tiled=True
    )
    over_x = jnp.sum(over_x, axis=0).reshape(4, 4, 8, full)
    over_l = lax.all_to_all(
        jnp.swapaxes(over_x, 0, 1), "zl", 0, 0, tiled=True
    )
    over_l = jnp.sum(over_l, axis=0)
    over_h = lax.all_to_all(over_l, "zh", 0, 0, tiled=True)
    own = jnp.sum(over_h, axis=0)
    back_h = lax.all_gather(own, "zh", axis=0, tiled=False)
    back_l = lax.all_gather(back_h, "zl", axis=1, tiled=False)
    back_z = back_l.reshape(1, 128, full)
    whole = lax.all_to_all(
        jnp.broadcast_to(back_z, (4, 128, full)), "x", 0, 0, tiled=True
    ).reshape(512, full)
    gram = join_cores(
        lax.all_gather(
            jnp.transpose(whole[:, width:]), "y", axis=0, tiled=True
        )
    )
    triangle, inverse = chol_inv(gram)
    basis_t = mxu(inverse, panel_t, ((1,), (0,)))
    coupling = mxu(inverse, whole[:, :width], ((1,), (0,)))
    projected = trailing - mxu(basis_t, coupling, ((0,), (0,)))
    row = 128 * lax.axis_index("x") + 32 * lax.axis_index("zh")
    row = row + 8 * lax.axis_index("zl")
    return (
        triangle,
        lax.dynamic_slice_in_dim(coupling, row, 8, axis=0),
        projected,
    )


def solution(mesh):
    fine = Mesh(
        mesh.devices.reshape(4, 4, 4, 4, 2), ("x", "zh", "zl", "y", "core")
    )
    cell, col = ("x", "zh", "zl"), ("y", "core")
    placed = P(cell, col)
    return jax.shard_map(
        on_device,
        mesh=fine,
        in_specs=(placed, placed),
        out_specs=(P(), placed, placed),
        check_vma=False,
    )
```

```python
import functools
import jax, jax.numpy as jnp
from jax import lax
from jax.sharding import Mesh
from jax.sharding import PartitionSpec as P
from jax.experimental import pallas as pl
from jax.experimental.pallas import tpu as pltpu

HI = lax.Precision.HIGHEST
NB = 128


def mxu(a, b, dims):
    return lax.dot_general(a, b, (dims, ((), ())), precision=HI, preferred_element_type=jnp.float32)


def factor_block(s_full, rows_ref):
    G = NB // 8
    sub = lax.broadcasted_iota(jnp.int32, (8, NB), 0)
    lane = lax.broadcasted_iota(jnp.int32, (8, NB), 1)
    s = [s_full[8 * g : 8 * g + 8, :] for g in range(G)]
    v = [jnp.where(lane == sub + 8 * g, 1.0, 0.0).astype(jnp.float32) for g in range(G)]
    for k in range(NB):
        g0, i0 = k // 8, k % 8
        col = [jnp.broadcast_to(s[g][:, k : k + 1], (8, NB)) for g in range(g0, G)]
        r = s[g0][i0 : i0 + 1, :]
        rows_ref[k : k + 1, :] = r
        if k == NB - 1:
            break
        inv = 1.0 / col[0][i0 : i0 + 1, :]
        rd = jnp.broadcast_to(r * inv, (8, NB))
        vd = jnp.broadcast_to(v[g0][i0 : i0 + 1, :] * inv, (8, NB))
        for g in range(g0, G):
            c = col[g - g0]
            if g == g0:
                if i0 == 7:
                    continue
                c = jnp.where(sub > i0, c, 0.0)
            s[g] = s[g] - c * rd
            v[g] = v[g] - c * vd
    return jnp.concatenate(v, axis=0)


def start_kernel(n, g_ref, a_ref):
    a_ref[:, :n] = g_ref[...]
    row = lax.broadcasted_iota(jnp.int32, (n, n), 0)
    a_ref[:, n:] = jnp.where(row == lax.broadcasted_iota(jnp.int32, (n, n), 1), 1.0, 0.0)


def steps_kernel(n, first, last, *refs):
    if first == 0:
        g_ref, a, rows = refs
        start_kernel(n, g_ref, a)
    else:
        _, a, rows = refs
    sub = lax.broadcasted_iota(jnp.int32, (NB, NB), 0)
    lane = lax.broadcasted_iota(jnp.int32, (NB, NB), 1)
    wide = lax.broadcasted_iota(jnp.int32, (NB, n), 1)
    high = lax.broadcasted_iota(jnp.int32, (NB, n), 0)
    tall = lax.broadcasted_iota(jnp.int32, (n, n), 0)

    def step(kb, carry):
        at = pl.multiple_of(kb * NB, NB)
        v = factor_block(a[pl.ds(at, NB), pl.ds(at, NB)], rows)
        rt = rows[...]
        d = jnp.sum(jnp.where(sub == lane, rt, 0.0), axis=1, keepdims=True)
        linv = v * lax.rsqrt(d)
        out = mxu(linv, a[pl.ds(at, NB), :], ((1,), (0,)))
        rm = jnp.where(wide >= at + NB, out[:, :n], 0.0)
        full = jnp.concatenate([rm, out[:, n:]], axis=1)
        a[...] -= mxu(rm, full, ((0,), (0,)))
        a[pl.ds(at, NB), n:] = out[:, n:]
        a[pl.ds(at, NB), :n] = jnp.where(wide >= at + high, out[:, :n], 0.0)
        return carry

    lax.fori_loop(first, last, step, 0)


def factor_steps(n, first, last, x):
    cost = pl.CostEstimate(
        flops=(last - first) * 2 * 6 * n * n * n // 2, bytes_accessed=4 * n * n * 4, transcendentals=0
    )
    return pl.pallas_call(
        functools.partial(steps_kernel, n, first, last),
        out_shape=jax.ShapeDtypeStruct((n, 2 * n), jnp.float32),
        in_specs=[pl.BlockSpec(memory_space=pltpu.VMEM)],
        out_specs=pl.BlockSpec(memory_space=pltpu.VMEM),
        scratch_shapes=[pltpu.VMEM((NB, NB), jnp.float32)],
        input_output_aliases={} if first == 0 else {0: 0},
        cost_estimate=cost,
        compiler_params=pltpu.CompilerParams(vmem_limit_bytes=32 << 20),
    )(x)


def join_cores(part):
    half = part.shape[0] // 2
    both = []
    for block in (part[:half], part[half:]):
        pair = lax.all_gather(block, "core", axis=0, tiled=False)
        both.append(jnp.swapaxes(pair.reshape(2, 2, 64, -1), 0, 1))
    return jnp.concatenate(both, axis=0).reshape(2 * part.shape[0], -1)


CELL = ("x", "z")


def exchange(blocks, axes):
    return lax.all_to_all(blocks, axes, 0, 0, tiled=True)


def on_device(panel_block, trailing):
    width = trailing.shape[1]
    block_t = jnp.transpose(panel_block)
    panel_t = join_cores(lax.all_gather(block_t, "y", axis=0, tiled=True))
    partial = mxu(panel_t, trailing, ((1,), (0,)))
    gram = mxu(block_t, panel_t, ((1,), (1,)))
    blocks, here = partial.reshape(4, 128, width), lax.axis_index("x")
    away = [
        lax.ppermute(
            lax.dynamic_index_in_dim(blocks, (here + k) % 4, 0, False),
            "x",
            [(i, (i + k) % 4) for i in range(4)],
        )
        for k in (1, 2, 3)
    ]
    c = lax.dynamic_index_in_dim(blocks, here, 0, False)
    c = (c + away[1]) + (away[0] + away[2])
    c = exchange(c.reshape(16, 8, width), "z")
    c = jnp.sum(c, axis=0)
    c = exchange(jnp.broadcast_to(c[None], (16, 8, width)), "z")
    c = exchange(jnp.broadcast_to(c.reshape(1, 128, width), (4, 128, width)), "x")
    c = c.reshape(512, width)
    gram = exchange(gram.reshape(64, 1, 512), CELL)
    gram = jnp.sum(gram, axis=0)
    gram = lax.all_gather(gram, "z", axis=0, tiled=False)
    gram = lax.all_gather(gram, "x", axis=0, tiled=False)
    gram = join_cores(lax.all_gather(gram.reshape(64, 512), "y", axis=0, tiled=True))
    state = factor_steps(512, 0, 2, gram)
    state = factor_steps(512, 2, 4, state)
    triangle, inverse = state[:, :512], state[:, 512:]
    basis_t = mxu(inverse, panel_t, ((1,), (0,)))
    coupling = mxu(inverse, c, ((1,), (0,)))
    projected = trailing - mxu(basis_t, coupling, ((0,), (0,)))
    row = 128 * lax.axis_index("x") + 8 * lax.axis_index("z")
    mine = lax.dynamic_slice_in_dim(coupling, row, 8, axis=0)
    return (triangle, mine, projected)


def solution(mesh):
    fine = Mesh(mesh.devices.reshape(4, 16, 4, 2), ("x", "z", "y", "core"))
    placed = P(CELL, ("y", "core"))
    return jax.shard_map(
        on_device,
        mesh=fine,
        in_specs=(placed, placed),
        out_specs=(P(), placed, placed),
        check_vma=False,
    )
```

```python
import functools
import jax, jax.numpy as jnp
from jax import lax
from jax.sharding import Mesh
from jax.sharding import PartitionSpec as P
from jax.experimental import pallas as pl
from jax.experimental.pallas import tpu as pltpu

HI = lax.Precision.HIGHEST
NB = 128


def mxu(a, b, dims):
    return lax.dot_general(a, b, (dims, ((), ())), precision=HI, preferred_element_type=jnp.float32)


def factor_block(s_full, rows_ref):
    groups = NB // 8
    sub = lax.broadcasted_iota(jnp.int32, (8, NB), 0)
    lane = lax.broadcasted_iota(jnp.int32, (8, NB), 1)

    def spread(row):
        return jnp.broadcast_to(row, (8, NB))

    s = [s_full[8 * g : 8 * g + 8, :] for g in range(groups)]
    v = [jnp.where(lane == sub + 8 * g, 1.0, 0.0).astype(jnp.float32) for g in range(groups)]
    for g0 in range(groups):
        at = 8 * g0
        cols = [jnp.broadcast_to(s[g0][:, at + m : at + m + 1], (8, NB)) for m in range(8)]
        u, w = s[g0], v[g0]
        inv_d = jnp.zeros((8, NB), jnp.float32)
        for j in range(8):
            inv = spread(1.0 / cols[j][j : j + 1, :])
            inv_d = jnp.where(sub == j, inv, inv_d)
            if j == 7:
                break
            mult = jnp.where(sub > j, cols[j] * inv, 0.0)
            for m in range(j + 1, 8):
                cols[m] = cols[m] - mult * spread(cols[m][j : j + 1, :])
            u = u - mult * spread(u[j : j + 1, :])
            w = w - mult * spread(w[j : j + 1, :])
        rows_ref[at : at + 8, :] = u
        v[g0] = w
        if g0 == groups - 1:
            break
        u, w = u * inv_d, w * inv_d
        for j in range(7, 0, -1):
            coef = jnp.where(sub < j, cols[j] * inv_d, 0.0)
            u = u - coef * spread(u[j : j + 1, :])
            w = w - coef * spread(w[j : j + 1, :])
        us = [spread(u[m : m + 1, :]) for m in range(8)]
        ws = [spread(w[m : m + 1, :]) for m in range(8)]
        for g in range(g0 + 1, groups):
            c = [jnp.broadcast_to(s[g][:, at + m : at + m + 1], (8, NB)) for m in range(8)]
            du = [c[m] * us[m] for m in range(8)]
            dw = [c[m] * ws[m] for m in range(8)]
            while len(du) > 1:
                du = [du[i] + du[i + 1] for i in range(0, len(du), 2)]
                dw = [dw[i] + dw[i + 1] for i in range(0, len(dw), 2)]
            s[g] = s[g] - du[0]
            v[g] = v[g] - dw[0]
    return jnp.concatenate(v, axis=0)


def start_kernel(n, g_ref, a_ref):
    a_ref[:, :n] = g_ref[...]
    row = lax.broadcasted_iota(jnp.int32, (n, n), 0)
    a_ref[:, n:] = jnp.where(row == lax.broadcasted_iota(jnp.int32, (n, n), 1), 1.0, 0.0)


def steps_kernel(n, first, last, *refs):
    if first == 0:
        g_ref, a, rows = refs
        start_kernel(n, g_ref, a)
    else:
        _, a, r_ref, x_ref, rows = refs
    sub = lax.broadcasted_iota(jnp.int32, (NB, NB), 0)
    lane = lax.broadcasted_iota(jnp.int32, (NB, NB), 1)
    wide = lax.broadcasted_iota(jnp.int32, (NB, n), 1)
    high = lax.broadcasted_iota(jnp.int32, (NB, n), 0)
    tall = lax.broadcasted_iota(jnp.int32, (n, n), 0)

    def step(kb, carry):
        at = pl.multiple_of(kb * NB, NB)
        v = factor_block(a[pl.ds(at, NB), pl.ds(at, NB)], rows)
        rt = rows[...]
        d = jnp.sum(jnp.where(sub == lane, rt, 0.0), axis=1, keepdims=True)
        linv = v * lax.rsqrt(d)
        out = mxu(linv, a[pl.ds(at, NB), :], ((1,), (0,)))
        rm = jnp.where(wide >= at + NB, out[:, :n], 0.0)
        full = jnp.concatenate([rm, out[:, n:]], axis=1)
        a[...] -= mxu(rm, full, ((0,), (0,)))
        a[pl.ds(at, NB), n:] = out[:, n:]
        a[pl.ds(at, NB), :n] = jnp.where(wide >= at + high, out[:, :n], 0.0)
        return carry

    lax.fori_loop(first, last, step, 0)
    if first:
        r_ref[...] = a[:, :n]
        x_ref[...] = a[:, n:]


def factor_steps(n, first, last, x):
    cost = pl.CostEstimate(
        flops=(last - first) * 2 * 6 * n * n * n // 2, bytes_accessed=4 * n * n * 4, transcendentals=0
    )
    state = jax.ShapeDtypeStruct((n, 2 * n), jnp.float32)
    half = jax.ShapeDtypeStruct((n, n), jnp.float32)
    outs = (state, half, half) if first else (state,)
    return pl.pallas_call(
        functools.partial(steps_kernel, n, first, last),
        out_shape=outs,
        in_specs=[pl.BlockSpec(memory_space=pltpu.VMEM)],
        out_specs=[pl.BlockSpec(memory_space=pltpu.VMEM)] * len(outs),
        scratch_shapes=[pltpu.VMEM((NB, NB), jnp.float32)],
        input_output_aliases={0: 0} if first else {},
        cost_estimate=cost,
        compiler_params=pltpu.CompilerParams(vmem_limit_bytes=32 << 20),
    )(x)


def join_cores(part):
    other = lax.ppermute(part, "core", [(0, 1), (1, 0)])
    first = lax.axis_index("core") == 0
    pair = (jnp.where(first, part, other), jnp.where(first, other, part))
    return jnp.stack(pair, axis=1).reshape(512, -1)


CELL = ("x", "z")


def exchange(blocks, axes):
    return lax.all_to_all(blocks, axes, 0, 0, tiled=True)


def on_device(panel_block, trailing):
    width = trailing.shape[1]
    block_t = jnp.transpose(panel_block)
    panel_t = join_cores(exchange(jnp.broadcast_to(block_t, (4, 64, 512)), "y"))
    partial = mxu(panel_t, trailing, ((1,), (0,)))
    gram = mxu(block_t, panel_t, ((1,), (1,)))
    blocks, here = partial.reshape(4, 128, width), lax.axis_index("x")
    away = [
        lax.ppermute(
            lax.dynamic_index_in_dim(blocks, (here + k) % 4, 0, False),
            "x",
            [(i, (i + k) % 4) for i in range(4)],
        )
        for k in (1, 2, 3)
    ]
    c = lax.dynamic_index_in_dim(blocks, here, 0, False)
    c = (c + away[1]) + (away[0] + away[2])
    c = exchange(c.reshape(16, 8, width), "z")
    c = jnp.sum(c, axis=0)
    c = lax.all_gather(c, "z", axis=0, tiled=True)
    c = exchange(jnp.broadcast_to(c.reshape(1, 128, width), (4, 128, width)), "x")
    c = c.reshape(512, width)
    gram = exchange(gram.reshape(64, 1, 512), CELL)
    gram = jnp.sum(gram, axis=0)
    gram = exchange(jnp.broadcast_to(gram, (64, 1, 512)), CELL)
    gram = lax.all_gather(gram.reshape(64, 512), "y", axis=0, tiled=False)
    gram = join_cores(gram)
    (state,) = factor_steps(512, 0, 2, gram)
    _, triangle, inverse = factor_steps(512, 2, 4, state)
    basis_t = mxu(inverse, panel_t, ((1,), (0,)))
    coupling = mxu(inverse, c, ((1,), (0,)))
    projected = trailing - mxu(basis_t, coupling, ((0,), (0,)))
    row = 128 * lax.axis_index("x") + 8 * lax.axis_index("z")
    mine = lax.dynamic_slice_in_dim(coupling, row, 8, axis=0)
    return (triangle, mine, projected)


def solution(mesh):
    fine = Mesh(mesh.devices.reshape(4, 16, 4, 2), ("x", "z", "y", "core"))
    placed = P(CELL, ("y", "core"))
    return jax.shard_map(
        on_device,
        mesh=fine,
        in_specs=(placed, placed),
        out_specs=(P(), placed, placed),
        check_vma=False,
    )
```

```python
import functools
import jax, jax.numpy as jnp
from jax import lax
from jax.sharding import Mesh
from jax.sharding import PartitionSpec as P
from jax.experimental import pallas as pl
from jax.experimental.pallas import tpu as pltpu

HI = lax.Precision.HIGHEST
NB = 128


def mxu(a, b, dims, precision=HI):
    return lax.dot_general(a, b, (dims, ((), ())), precision=precision, preferred_element_type=jnp.float32)


def factor_block(s_full, rows_ref):
    groups = NB // 8
    sub = lax.broadcasted_iota(jnp.int32, (8, NB), 0)
    lane = lax.broadcasted_iota(jnp.int32, (8, NB), 1)

    def spread(row):
        return jnp.broadcast_to(row, (8, NB))

    s = [s_full[8 * g : 8 * g + 8, :] for g in range(groups)]
    v = [jnp.where(lane == sub + 8 * g, 1.0, 0.0).astype(jnp.float32) for g in range(groups)]
    for g0 in range(groups):
        at = 8 * g0
        cols = [jnp.broadcast_to(s[g0][:, at + m : at + m + 1], (8, NB)) for m in range(8)]
        u, w = s[g0], v[g0]
        inv_d = jnp.zeros((8, NB), jnp.float32)
        for j in range(8):
            inv = spread(1.0 / cols[j][j : j + 1, :])
            inv_d = jnp.where(sub == j, inv, inv_d)
            if j == 7:
                break
            mult = jnp.where(sub > j, cols[j] * inv, 0.0)
            for m in range(j + 1, 8):
                cols[m] = cols[m] - mult * spread(cols[m][j : j + 1, :])
            u = u - mult * spread(u[j : j + 1, :])
            w = w - mult * spread(w[j : j + 1, :])
        rows_ref[at : at + 8, :] = u
        v[g0] = w
        if g0 == groups - 1:
            break
        u, w = u * inv_d, w * inv_d
        for j in range(7, 0, -1):
            coef = jnp.where(sub < j, cols[j] * inv_d, 0.0)
            u = u - coef * spread(u[j : j + 1, :])
            w = w - coef * spread(w[j : j + 1, :])
        us = [spread(u[m : m + 1, :]) for m in range(8)]
        ws = [spread(w[m : m + 1, :]) for m in range(8)]
        for g in range(g0 + 1, groups):
            c = [jnp.broadcast_to(s[g][:, at + m : at + m + 1], (8, NB)) for m in range(8)]
            du = [c[m] * us[m] for m in range(8)]
            dw = [c[m] * ws[m] for m in range(8)]
            while len(du) > 1:
                du = [du[i] + du[i + 1] for i in range(0, len(du), 2)]
                dw = [dw[i] + dw[i + 1] for i in range(0, len(dw), 2)]
            s[g] = s[g] - du[0]
            v[g] = v[g] - dw[0]
    return jnp.concatenate(v, axis=0)


def start_kernel(n, g_ref, a_ref):
    a_ref[:, :n] = g_ref[...]
    row = lax.broadcasted_iota(jnp.int32, (n, n), 0)
    a_ref[:, n:] = jnp.where(row == lax.broadcasted_iota(jnp.int32, (n, n), 1), 1.0, 0.0)


def steps_kernel(n, first, last, *refs):
    if first == 0:
        g_ref, a, rows = refs
        start_kernel(n, g_ref, a)
    else:
        _, a, r_ref, x_ref, rows = refs
    sub = lax.broadcasted_iota(jnp.int32, (NB, NB), 0)
    lane = lax.broadcasted_iota(jnp.int32, (NB, NB), 1)
    wide = lax.broadcasted_iota(jnp.int32, (NB, n), 1)
    high = lax.broadcasted_iota(jnp.int32, (NB, n), 0)
    tall = lax.broadcasted_iota(jnp.int32, (n, n), 0)

    def step(kb, carry):
        at = pl.multiple_of(kb * NB, NB)
        v = factor_block(a[pl.ds(at, NB), pl.ds(at, NB)], rows)
        rt = rows[...]
        d = jnp.sum(jnp.where(sub == lane, rt, 0.0), axis=1, keepdims=True)
        linv = v * lax.rsqrt(d)
        out = mxu(linv, a[pl.ds(at, NB), :], ((1,), (0,)))
        rm = jnp.where(wide >= at + NB, out[:, :n], 0.0)
        full = jnp.concatenate([rm, out[:, n:]], axis=1)
        a[...] -= mxu(rm, full, ((0,), (0,)))
        a[pl.ds(at, NB), n:] = out[:, n:]
        a[pl.ds(at, NB), :n] = jnp.where(wide >= at + high, out[:, :n], 0.0)
        return carry

    lax.fori_loop(first, last, step, 0)
    if first:
        r_ref[...] = a[:, :n]
        x_ref[...] = a[:, n:]


def factor_steps(n, first, last, x):
    cost = pl.CostEstimate(
        flops=(last - first) * 2 * 6 * n * n * n // 2, bytes_accessed=4 * n * n * 4, transcendentals=0
    )
    state = jax.ShapeDtypeStruct((n, 2 * n), jnp.float32)
    half = jax.ShapeDtypeStruct((n, n), jnp.float32)
    outs = (state, half, half) if first else (state,)
    return pl.pallas_call(
        functools.partial(steps_kernel, n, first, last),
        out_shape=outs,
        in_specs=[pl.BlockSpec(memory_space=pltpu.VMEM)],
        out_specs=[pl.BlockSpec(memory_space=pltpu.VMEM)] * len(outs),
        scratch_shapes=[pltpu.VMEM((NB, NB), jnp.float32)],
        input_output_aliases={0: 0} if first else {},
        cost_estimate=cost,
        compiler_params=pltpu.CompilerParams(vmem_limit_bytes=32 << 20),
    )(x)


def join_cores(part):
    other = lax.ppermute(part, "core", [(0, 1), (1, 0)])
    first = lax.axis_index("core") == 0
    pair = (jnp.where(first, part, other), jnp.where(first, other, part))
    return jnp.stack(pair, axis=1).reshape(512, -1)


CELL = ("x", "z")


def exchange(blocks, axes):
    return lax.all_to_all(blocks, axes, 0, 0, tiled=True)


def on_device(panel_block, trailing):
    width = trailing.shape[1]
    block_t = jnp.transpose(panel_block)
    panel_t = join_cores(exchange(jnp.broadcast_to(block_t, (4, 64, 512)), "y"))
    partial = mxu(panel_t, trailing, ((1,), (0,)))
    gram = mxu(block_t, panel_t, ((1,), (1,)))
    blocks, here = partial.reshape(4, 128, width), lax.axis_index("x")
    away = [
        lax.ppermute(
            lax.dynamic_index_in_dim(blocks, (here + k) % 4, 0, False),
            "x",
            [(i, (i + k) % 4) for i in range(4)],
        )
        for k in (1, 2, 3)
    ]
    c = lax.dynamic_index_in_dim(blocks, here, 0, False)
    c = (c + away[1]) + (away[0] + away[2])
    c = exchange(c.reshape(16, 8, width), "z")
    c = jnp.sum(c, axis=0)
    c = exchange(jnp.broadcast_to(c, (16, 8, width)), "z")
    c = exchange(jnp.broadcast_to(c.reshape(1, 128, width), (4, 128, width)), "x")
    c = c.reshape(512, width)
    gram = exchange(gram.reshape(4, 16, 512), "x")
    gram = jnp.sum(gram, axis=0)
    gram = exchange(gram.reshape(16, 1, 512), "z")
    gram = jnp.sum(gram, axis=0)
    gram = exchange(jnp.broadcast_to(gram, (16, 1, 512)), "z")
    gram = exchange(jnp.broadcast_to(gram.reshape(1, 16, 512), (4, 16, 512)), "x")
    gram = lax.all_gather(gram.reshape(64, 512), "y", axis=0, tiled=False)
    gram = join_cores(gram)
    (state,) = factor_steps(512, 0, 2, gram)
    _, triangle, inverse = factor_steps(512, 2, 4, state)
    basis_t = mxu(inverse, panel_t, ((1,), (0,)))
    coupling = mxu(inverse, c, ((1,), (0,)))
    projected = trailing - mxu(basis_t, coupling, ((0,), (0,)), lax.Precision.HIGH)
    row = 128 * lax.axis_index("x") + 8 * lax.axis_index("z")
    mine = lax.dynamic_slice_in_dim(coupling, row, 8, axis=0)
    return (triangle, mine, projected)


def solution(mesh):
    fine = Mesh(mesh.devices.reshape(4, 16, 4, 2), ("x", "z", "y", "core"))
    placed = P(CELL, ("y", "core"))
    return jax.shard_map(
        on_device,
        mesh=fine,
        in_specs=(placed, placed),
        out_specs=(P(), placed, placed),
        check_vma=False,
    )
```

```python
import functools
import jax, jax.numpy as jnp
from jax import lax
from jax.sharding import Mesh
from jax.sharding import PartitionSpec as P
from jax.experimental import pallas as pl
from jax.experimental.pallas import tpu as pltpu

HI = lax.Precision.HIGHEST
NB = 128


def mxu(a, b, dims, precision=HI):
    return lax.dot_general(a, b, (dims, ((), ())), precision=precision, preferred_element_type=jnp.float32)


def factor_block(s_full, rows_ref):
    groups = NB // 8
    sub = lax.broadcasted_iota(jnp.int32, (8, NB), 0)
    lane = lax.broadcasted_iota(jnp.int32, (8, NB), 1)

    def spread(row):
        return jnp.broadcast_to(row, (8, NB))

    s = [s_full[8 * g : 8 * g + 8, :] for g in range(groups)]
    v = [jnp.where(lane == sub + 8 * g, 1.0, 0.0).astype(jnp.float32) for g in range(groups)]
    for g0 in range(groups):
        at = 8 * g0
        cols = [jnp.broadcast_to(s[g0][:, at + m : at + m + 1], (8, NB)) for m in range(8)]
        u, w = s[g0], v[g0]
        inv_d = jnp.zeros((8, NB), jnp.float32)
        for j in range(8):
            inv = spread(1.0 / cols[j][j : j + 1, :])
            inv_d = jnp.where(sub == j, inv, inv_d)
            if j == 7:
                break
            mult = jnp.where(sub > j, cols[j] * inv, 0.0)
            for m in range(j + 1, 8):
                cols[m] = cols[m] - mult * spread(cols[m][j : j + 1, :])
            u = u - mult * spread(u[j : j + 1, :])
            w = w - mult * spread(w[j : j + 1, :])
        rows_ref[at : at + 8, :] = u
        v[g0] = w
        if g0 == groups - 1:
            break
        u, w = u * inv_d, w * inv_d
        for j in range(7, 0, -1):
            coef = jnp.where(sub < j, cols[j] * inv_d, 0.0)
            u = u - coef * spread(u[j : j + 1, :])
            w = w - coef * spread(w[j : j + 1, :])
        us = [spread(u[m : m + 1, :]) for m in range(8)]
        ws = [spread(w[m : m + 1, :]) for m in range(8)]
        for g in range(g0 + 1, groups):
            c = [jnp.broadcast_to(s[g][:, at + m : at + m + 1], (8, NB)) for m in range(8)]
            du = [c[m] * us[m] for m in range(8)]
            dw = [c[m] * ws[m] for m in range(8)]
            while len(du) > 1:
                du = [du[i] + du[i + 1] for i in range(0, len(du), 2)]
                dw = [dw[i] + dw[i + 1] for i in range(0, len(dw), 2)]
            s[g] = s[g] - du[0]
            v[g] = v[g] - dw[0]
    return jnp.concatenate(v, axis=0)


def block_row(n, c, a, linv):
    at, to = c * NB, (c + 1) * NB
    upper = lax.broadcasted_iota(jnp.int32, (NB, NB), 0) <= lax.broadcasted_iota(jnp.int32, (NB, NB), 1)
    right = mxu(linv, a[at:to, at:n], ((1,), (0,)))
    left = [mxu(linv, a[at:to, n : n + at], ((1,), (0,)))] if c else []
    if to < n:
        below = mxu(a[to:n, at:to], linv, ((1,), (1,)))
        a[to:n, to:n] -= mxu(below, right[:, NB:], ((1,), (0,)))
        if c:
            a[to:n, n : n + at] -= mxu(below, left[0], ((1,), (0,)))
        a[to:n, n + at : n + to] = -mxu(below, linv, ((1,), (0,)))
        a[at:to, to:n] = right[:, NB:]
        a[at:to, n + to : 2 * n] = jnp.zeros((NB, n - to), jnp.float32)
    if c:
        a[at:to, :at] = jnp.zeros((NB, at), jnp.float32)
        a[at:to, n : n + at] = left[0]
    a[at:to, at:to] = jnp.where(upper, right[:, :NB], 0.0)
    a[at:to, n + at : n + to] = linv


def steps_kernel(n, first, last, *refs):
    if first == 0:
        g_ref, a, rows = refs
        a[:, :n] = g_ref[...]
    else:
        _, a, r_ref, x_ref, rows = refs
    sub = lax.broadcasted_iota(jnp.int32, (NB, NB), 0)
    lane = lax.broadcasted_iota(jnp.int32, (NB, NB), 1)

    def step(kb, carry):
        at = pl.multiple_of(kb * NB, NB)
        v = factor_block(a[pl.ds(at, NB), pl.ds(at, NB)], rows)
        d = jnp.sum(jnp.where(sub == lane, rows[...], 0.0), axis=1, keepdims=True)
        rows[...] = v * lax.rsqrt(d)
        for c in range(first, last):
            pl.when(kb == c)(lambda c=c: block_row(n, c, a, rows[...]))
        return carry

    lax.fori_loop(first, last, step, 0)
    if first:
        r_ref[...] = a[:, :n]
        x_ref[...] = a[:, n:]


def factor_steps(n, first, last, x):
    cost = pl.CostEstimate(
        flops=(last - first) * 2 * 6 * n * n * n // 2, bytes_accessed=4 * n * n * 4, transcendentals=0
    )
    state = jax.ShapeDtypeStruct((n, 2 * n), jnp.float32)
    half = jax.ShapeDtypeStruct((n, n), jnp.float32)
    outs = (state, half, half) if first else (state,)
    return pl.pallas_call(
        functools.partial(steps_kernel, n, first, last),
        out_shape=outs,
        in_specs=[pl.BlockSpec(memory_space=pltpu.VMEM)],
        out_specs=[pl.BlockSpec(memory_space=pltpu.VMEM)] * len(outs),
        scratch_shapes=[pltpu.VMEM((NB, NB), jnp.float32)],
        input_output_aliases={0: 0} if first else {},
        cost_estimate=cost,
        compiler_params=pltpu.CompilerParams(vmem_limit_bytes=16 << 20),
    )(x)


def join_cores(part):
    other = lax.ppermute(part, "core", [(0, 1), (1, 0)])
    first = lax.axis_index("core") == 0
    pair = (jnp.where(first, part, other), jnp.where(first, other, part))
    return jnp.stack(pair, axis=1).reshape(512, -1)


CELL = ("x", "z")


def exchange(blocks, axes):
    return lax.all_to_all(blocks, axes, 0, 0, tiled=True)


def on_device(panel_block, trailing):
    width = trailing.shape[1]
    block_t = jnp.transpose(panel_block)
    panel_t = join_cores(exchange(jnp.broadcast_to(block_t, (4, 64, 512)), "y"))
    partial = mxu(panel_t, trailing, ((1,), (0,)))
    gram = mxu(block_t, panel_t, ((1,), (1,)))
    blocks, here = partial.reshape(4, 128, width), lax.axis_index("x")
    away = [
        lax.ppermute(
            lax.dynamic_index_in_dim(blocks, (here + k) % 4, 0, False),
            "x",
            [(i, (i + k) % 4) for i in range(4)],
        )
        for k in (1, 2, 3)
    ]
    c = lax.dynamic_index_in_dim(blocks, here, 0, False)
    c = (c + away[1]) + (away[0] + away[2])
    c = exchange(c.reshape(16, 8, width), "z")
    c = jnp.sum(c, axis=0)
    c = lax.all_gather(c, "z", axis=0, tiled=True)
    c = exchange(jnp.broadcast_to(c.reshape(1, 128, width), (4, 128, width)), "x")
    c = c.reshape(512, width)
    gram = exchange(gram.reshape(64, 1, 512), CELL)
    gram = jnp.sum(gram, axis=0)
    gram = exchange(jnp.broadcast_to(gram, (64, 1, 512)), CELL)
    gram = lax.all_gather(gram.reshape(64, 512), "y", axis=0, tiled=False)
    gram = join_cores(gram)
    (state,) = factor_steps(512, 0, 2, gram)
    _, triangle, inverse = factor_steps(512, 2, 4, state)
    basis_t = mxu(inverse, panel_t, ((1,), (0,)))
    coupling = mxu(inverse, c, ((1,), (0,)))
    projected = trailing - mxu(basis_t, coupling, ((0,), (0,)), lax.Precision.HIGH)
    row = 128 * lax.axis_index("x") + 8 * lax.axis_index("z")
    mine = lax.dynamic_slice_in_dim(coupling, row, 8, axis=0)
    return (triangle, mine, projected)


def solution(mesh):
    fine = Mesh(mesh.devices.reshape(4, 16, 4, 2), ("x", "z", "y", "core"))
    placed = P(CELL, ("y", "core"))
    return jax.shard_map(
        on_device,
        mesh=fine,
        in_specs=(placed, placed),
        out_specs=(P(), placed, placed),
        check_vma=False,
    )
```

```python
import functools
import jax, jax.numpy as jnp
from jax import lax
from jax.sharding import Mesh
from jax.sharding import PartitionSpec as P
from jax.experimental import pallas as pl
from jax.experimental.pallas import tpu as pltpu

HI = lax.Precision.HIGHEST
NB = 128


def mxu(a, b, dims, precision=HI):
    return lax.dot_general(a, b, (dims, ((), ())), precision=precision, preferred_element_type=jnp.float32)


def factor_block(s_full, rows_ref):
    groups = NB // 8
    sub = lax.broadcasted_iota(jnp.int32, (8, NB), 0)
    lane = lax.broadcasted_iota(jnp.int32, (8, NB), 1)

    def spread(row):
        return jnp.broadcast_to(row, (8, NB))

    s = [s_full[8 * g : 8 * g + 8, :] for g in range(groups)]
    v = [jnp.where(lane == sub + 8 * g, 1.0, 0.0).astype(jnp.float32) for g in range(groups)]
    for g0 in range(groups):
        at = 8 * g0
        cols = [jnp.broadcast_to(s[g0][:, at + m : at + m + 1], (8, NB)) for m in range(8)]
        u, w = s[g0], v[g0]
        inv_d = jnp.zeros((8, NB), jnp.float32)
        for j in range(8):
            inv = spread(1.0 / cols[j][j : j + 1, :])
            inv_d = jnp.where(sub == j, inv, inv_d)
            if j == 7:
                break
            mult = jnp.where(sub > j, cols[j] * inv, 0.0)
            for m in range(j + 1, 8):
                cols[m] = cols[m] - mult * spread(cols[m][j : j + 1, :])
            u = u - mult * spread(u[j : j + 1, :])
            w = w - mult * spread(w[j : j + 1, :])
        rows_ref[at : at + 8, :] = u
        v[g0] = w
        if g0 == groups - 1:
            break
        u, w = u * inv_d, w * inv_d
        for j in range(7, 0, -1):
            coef = jnp.where(sub < j, cols[j] * inv_d, 0.0)
            u = u - coef * spread(u[j : j + 1, :])
            w = w - coef * spread(w[j : j + 1, :])
        us = [spread(u[m : m + 1, :]) for m in range(8)]
        ws = [spread(w[m : m + 1, :]) for m in range(8)]
        for g in range(g0 + 1, groups):
            c = [jnp.broadcast_to(s[g][:, at + m : at + m + 1], (8, NB)) for m in range(8)]
            du = [c[m] * us[m] for m in range(8)]
            dw = [c[m] * ws[m] for m in range(8)]
            while len(du) > 1:
                du = [du[i] + du[i + 1] for i in range(0, len(du), 2)]
                dw = [dw[i] + dw[i + 1] for i in range(0, len(dw), 2)]
            s[g] = s[g] - du[0]
            v[g] = v[g] - dw[0]
    return jnp.concatenate(v, axis=0)


def block_row(n, c, a, linv):
    at, to = c * NB, (c + 1) * NB
    upper = lax.broadcasted_iota(jnp.int32, (NB, NB), 0) <= lax.broadcasted_iota(jnp.int32, (NB, NB), 1)
    right = mxu(linv, a[at:to, at:n], ((1,), (0,)))
    left = [mxu(linv, a[at:to, n : n + at], ((1,), (0,)))] if c else []
    if to < n:
        below = mxu(a[to:n, at:to], linv, ((1,), (1,)))
        a[to:n, to:n] -= mxu(below, right[:, NB:], ((1,), (0,)))
        if c:
            a[to:n, n : n + at] -= mxu(below, left[0], ((1,), (0,)))
        a[to:n, n + at : n + to] = -mxu(below, linv, ((1,), (0,)))
        a[at:to, to:n] = right[:, NB:]
        a[at:to, n + to : 2 * n] = jnp.zeros((NB, n - to), jnp.float32)
    if c:
        a[at:to, :at] = jnp.zeros((NB, at), jnp.float32)
        a[at:to, n : n + at] = left[0]
    a[at:to, at:to] = jnp.where(upper, right[:, :NB], 0.0)
    a[at:to, n + at : n + to] = linv


def steps_kernel(n, first, last, *refs):
    if first == 0:
        g_ref, a, rows = refs
        a[:, :n] = g_ref[...]
    else:
        a_in, r_ref, x_ref, a, rows = refs
        done = first * NB
        r_ref[:done, :] = a_in[:done, :n]
        x_ref[:done, :] = a_in[:done, n:]
        a[done:, :] = a_in[done:, :]
    sub = lax.broadcasted_iota(jnp.int32, (NB, NB), 0)
    lane = lax.broadcasted_iota(jnp.int32, (NB, NB), 1)

    def step(kb, carry):
        at = pl.multiple_of(kb * NB, NB)
        v = factor_block(a[pl.ds(at, NB), pl.ds(at, NB)], rows)
        d = jnp.sum(jnp.where(sub == lane, rows[...], 0.0), axis=1, keepdims=True)
        rows[...] = v * lax.rsqrt(d)
        for c in range(first, last):
            pl.when(kb == c)(lambda c=c: block_row(n, c, a, rows[...]))
        return carry

    lax.fori_loop(first, last, step, 0)
    if first:
        r_ref[done:, :] = a[done:, :n]
        x_ref[done:, :] = a[done:, n:]


def factor_steps(n, first, last, x):
    cost = pl.CostEstimate(
        flops=(last - first) * 2 * 6 * n * n * n // 2, bytes_accessed=4 * n * n * 4, transcendentals=0
    )
    state = jax.ShapeDtypeStruct((n, 2 * n), jnp.float32)
    half = jax.ShapeDtypeStruct((n, n), jnp.float32)
    outs = (half, half) if first else (state,)
    held = [pltpu.VMEM((n, 2 * n), jnp.float32)] if first else []
    return pl.pallas_call(
        functools.partial(steps_kernel, n, first, last),
        out_shape=outs,
        in_specs=[pl.BlockSpec(memory_space=pltpu.VMEM)],
        out_specs=[pl.BlockSpec(memory_space=pltpu.VMEM)] * len(outs),
        scratch_shapes=held + [pltpu.VMEM((NB, NB), jnp.float32)],
        cost_estimate=cost,
        compiler_params=pltpu.CompilerParams(vmem_limit_bytes=16 << 20),
    )(x)


def join_cores(part):
    other = lax.ppermute(part, "core", [(0, 1), (1, 0)])
    first = lax.axis_index("core") == 0
    pair = (jnp.where(first, part, other), jnp.where(first, other, part))
    return jnp.stack(pair, axis=1).reshape(512, -1)


CELL = ("x", "z")


def exchange(blocks, axes):
    return lax.all_to_all(blocks, axes, 0, 0, tiled=True)


def on_device(panel_block, trailing):
    width = trailing.shape[1]
    block_t = jnp.transpose(panel_block)
    panel_t = join_cores(exchange(jnp.broadcast_to(block_t, (4, 64, 512)), "y"))
    partial = mxu(panel_t, trailing, ((1,), (0,)))
    gram = mxu(block_t, panel_t, ((1,), (1,)))
    gram, partial = lax.optimization_barrier((gram, partial))
    blocks, here = partial.reshape(4, 128, width), lax.axis_index("x")
    away = {}
    for k in (2, 3, 1):
        away[k] = lax.ppermute(
            lax.dynamic_index_in_dim(blocks, (here + k) % 4, 0, False),
            "x",
            [(i, (i + k) % 4) for i in range(4)],
        )
    c = lax.dynamic_index_in_dim(blocks, here, 0, False)
    c = (c + away[2]) + (away[1] + away[3])
    c = exchange(c.reshape(16, 8, width), "z")
    c = jnp.sum(c, axis=0)
    c = lax.all_gather(c, "z", axis=0, tiled=True)
    c = exchange(jnp.broadcast_to(c.reshape(1, 128, width), (4, 128, width)), "x")
    c = c.reshape(512, width)
    gram = exchange(gram.reshape(64, 1, 512), CELL)
    gram = jnp.sum(gram, axis=0)
    gram = exchange(jnp.broadcast_to(gram, (64, 1, 512)), CELL)
    gram = lax.all_gather(gram.reshape(64, 512), "y", axis=0, tiled=False)
    gram = join_cores(gram)
    (state,) = factor_steps(512, 0, 2, gram)
    triangle, inverse = factor_steps(512, 2, 4, state)
    basis_t = mxu(inverse, panel_t, ((1,), (0,)))
    coupling = mxu(inverse, c, ((1,), (0,)))
    projected = trailing - mxu(basis_t, coupling, ((0,), (0,)), lax.Precision.HIGH)
    row = 128 * lax.axis_index("x") + 8 * lax.axis_index("z")
    mine = lax.dynamic_slice_in_dim(coupling, row, 8, axis=0)
    return (triangle, mine, projected)


def solution(mesh):
    fine = Mesh(mesh.devices.reshape(4, 16, 4, 2), ("x", "z", "y", "core"))
    placed = P(CELL, ("y", "core"))
    return jax.shard_map(
        on_device,
        mesh=fine,
        in_specs=(placed, placed),
        out_specs=(P(), placed, placed),
        check_vma=False,
    )
```

```python
import functools
import jax, jax.numpy as jnp
from jax import lax
from jax.sharding import Mesh
from jax.sharding import PartitionSpec as P
from jax.experimental import pallas as pl
from jax.experimental.pallas import tpu as pltpu

HI = lax.Precision.HIGHEST
NB = 128


def mxu(a, b, dims, precision=HI):
    return lax.dot_general(a, b, (dims, ((), ())), precision=precision, preferred_element_type=jnp.float32)


def factor_block(s_full, rows_ref):
    groups = NB // 8
    sub = lax.broadcasted_iota(jnp.int32, (8, NB), 0)
    lane = lax.broadcasted_iota(jnp.int32, (8, NB), 1)

    def spread(row):
        return jnp.broadcast_to(row, (8, NB))

    s = [s_full[8 * g : 8 * g + 8, :] for g in range(groups)]
    v = [jnp.where(lane == sub + 8 * g, 1.0, 0.0).astype(jnp.float32) for g in range(groups)]
    for g0 in range(groups):
        at = 8 * g0
        cols = [jnp.broadcast_to(s[g0][:, at + m : at + m + 1], (8, NB)) for m in range(8)]
        u, w = s[g0], v[g0]
        inv_d = jnp.zeros((8, NB), jnp.float32)
        for j in range(8):
            inv = spread(1.0 / cols[j][j : j + 1, :])
            inv_d = jnp.where(sub == j, inv, inv_d)
            if j == 7:
                break
            mult = jnp.where(sub > j, cols[j] * inv, 0.0)
            for m in range(j + 1, 8):
                cols[m] = cols[m] - mult * spread(cols[m][j : j + 1, :])
            u = u - mult * spread(u[j : j + 1, :])
            w = w - mult * spread(w[j : j + 1, :])
        rows_ref[at : at + 8, :] = u
        v[g0] = w
        if g0 == groups - 1:
            break
        u, w = u * inv_d, w * inv_d
        for j in range(7, 0, -1):
            coef = jnp.where(sub < j, cols[j] * inv_d, 0.0)
            u = u - coef * spread(u[j : j + 1, :])
            w = w - coef * spread(w[j : j + 1, :])
        us = [spread(u[m : m + 1, :]) for m in range(8)]
        ws = [spread(w[m : m + 1, :]) for m in range(8)]
        for g in range(g0 + 1, groups):
            c = [jnp.broadcast_to(s[g][:, at + m : at + m + 1], (8, NB)) for m in range(8)]
            du = [c[m] * us[m] for m in range(8)]
            dw = [c[m] * ws[m] for m in range(8)]
            while len(du) > 1:
                du = [du[i] + du[i + 1] for i in range(0, len(du), 2)]
                dw = [dw[i] + dw[i + 1] for i in range(0, len(dw), 2)]
            s[g] = s[g] - du[0]
            v[g] = v[g] - dw[0]
    return jnp.concatenate(v, axis=0)


def block_row(n, c, a, linv):
    at, to = c * NB, (c + 1) * NB
    upper = lax.broadcasted_iota(jnp.int32, (NB, NB), 0) <= lax.broadcasted_iota(jnp.int32, (NB, NB), 1)
    right = mxu(linv, a[at:to, at:n], ((1,), (0,)))
    left = [mxu(linv, a[at:to, n : n + at], ((1,), (0,)))] if c else []
    if to < n:
        below = mxu(a[to:n, at:to], linv, ((1,), (1,)))
        a[to:n, to:n] -= mxu(below, right[:, NB:], ((1,), (0,)))
        if c:
            a[to:n, n : n + at] -= mxu(below, left[0], ((1,), (0,)))
        a[to:n, n + at : n + to] = -mxu(below, linv, ((1,), (0,)))
        a[at:to, to:n] = right[:, NB:]
        a[at:to, n + to : 2 * n] = jnp.zeros((NB, n - to), jnp.float32)
    if c:
        a[at:to, :at] = jnp.zeros((NB, at), jnp.float32)
        a[at:to, n : n + at] = left[0]
    a[at:to, at:to] = jnp.where(upper, right[:, :NB], 0.0)
    a[at:to, n + at : n + to] = linv


def steps_kernel(n, first, last, *refs):
    if first == 0:
        g_ref, a, rows = refs
        a[:, :n] = g_ref[...]
    else:
        a_in, r_ref, x_ref, a, rows = refs
        done = first * NB
        r_ref[:done, :] = a_in[:done, :n]
        x_ref[:done, :] = a_in[:done, n:]
        a[done:, :] = a_in[done:, :]
    sub = lax.broadcasted_iota(jnp.int32, (NB, NB), 0)
    lane = lax.broadcasted_iota(jnp.int32, (NB, NB), 1)

    def step(kb, carry):
        at = pl.multiple_of(kb * NB, NB)
        v = factor_block(a[pl.ds(at, NB), pl.ds(at, NB)], rows)
        d = jnp.sum(jnp.where(sub == lane, rows[...], 0.0), axis=1, keepdims=True)
        rows[...] = v * lax.rsqrt(d)
        for c in range(first, last):
            pl.when(kb == c)(lambda c=c: block_row(n, c, a, rows[...]))
        return carry

    lax.fori_loop(first, last, step, 0)
    if first:
        r_ref[done:, :] = a[done:, :n]
        x_ref[done:, :] = a[done:, n:]


def factor_steps(n, first, last, x):
    cost = pl.CostEstimate(
        flops=(last - first) * 2 * 6 * n * n * n // 2, bytes_accessed=4 * n * n * 4, transcendentals=0
    )
    state = jax.ShapeDtypeStruct((n, 2 * n), jnp.float32)
    half = jax.ShapeDtypeStruct((n, n), jnp.float32)
    outs = (half, half) if first else (state,)
    held = [pltpu.VMEM((n, 2 * n), jnp.float32)] if first else []
    return pl.pallas_call(
        functools.partial(steps_kernel, n, first, last),
        out_shape=outs,
        in_specs=[pl.BlockSpec(memory_space=pltpu.VMEM)],
        out_specs=[pl.BlockSpec(memory_space=pltpu.VMEM)] * len(outs),
        scratch_shapes=held + [pltpu.VMEM((NB, NB), jnp.float32)],
        cost_estimate=cost,
        compiler_params=pltpu.CompilerParams(vmem_limit_bytes=16 << 20),
    )(x)


def join_cores(part):
    other = lax.ppermute(part, "core", [(0, 1), (1, 0)])
    first = lax.axis_index("core") == 0
    pair = (jnp.where(first, part, other), jnp.where(first, other, part))
    return jnp.stack(pair, axis=1).reshape(512, -1)


CELL = ("x", "z")


def exchange(blocks, axes):
    return lax.all_to_all(blocks, axes, 0, 0, tiled=True)


def on_device(panel_block, trailing):
    width = trailing.shape[1]
    block_t = jnp.transpose(panel_block)
    panel_t = join_cores(exchange(jnp.broadcast_to(block_t, (4, 64, 512)), "y"))
    partial = mxu(panel_t, trailing, ((1,), (0,)))
    gram = mxu(block_t, panel_t, ((1,), (1,)))
    blocks, here = partial.reshape(4, 128, width), lax.axis_index("x")
    away = [
        lax.ppermute(
            lax.dynamic_index_in_dim(blocks, (here + k) % 4, 0, False),
            "x",
            [(i, (i + k) % 4) for i in range(4)],
        )
        for k in (1, 2, 3)
    ]
    c = lax.dynamic_index_in_dim(blocks, here, 0, False)
    c = (c + away[1]) + (away[0] + away[2])
    c = exchange(c.reshape(16, 8, width), "z")
    c = jnp.sum(c, axis=0)
    c = lax.all_gather(c, "z", axis=0, tiled=True)
    c = exchange(jnp.broadcast_to(c.reshape(1, 128, width), (4, 128, width)), "x")
    c = c.reshape(512, width)
    gram = exchange(gram.reshape(64, 1, 512), CELL)
    gram = jnp.sum(gram, axis=0)
    gram = exchange(jnp.broadcast_to(gram, (64, 1, 512)), CELL)
    gram = lax.all_gather(gram.reshape(64, 512), "y", axis=0, tiled=False)
    gram = join_cores(gram)
    (state,) = factor_steps(512, 0, 2, gram)
    triangle, inverse = factor_steps(512, 2, 4, state)
    basis_t = mxu(inverse, panel_t, ((1,), (0,)))
    coupling = mxu(inverse, c, ((1,), (0,)))
    projected = trailing - mxu(basis_t, coupling, ((0,), (0,)), lax.Precision.HIGH)
    row = 128 * lax.axis_index("x") + 8 * lax.axis_index("z")
    mine = lax.dynamic_slice_in_dim(coupling, row, 8, axis=0)
    return (triangle, mine, projected)


def solution(mesh):
    fine = Mesh(mesh.devices.reshape(4, 16, 4, 2), ("x", "z", "y", "core"))
    placed = P(CELL, ("y", "core"))
    return jax.shard_map(
        on_device,
        mesh=fine,
        in_specs=(placed, placed),
        out_specs=(P(), placed, placed),
        check_vma=False,
    )
```
